32 devices in a mesh: section: 2 (over core), expert: 8 (over z, x), head: 2 (over y).
Axes of the slice: x: 2, y: 2, z: 4, core: 2. Of those that a mesh axis runs over, the one named last changes fastest.
Arguments:
- boundary: bfloat16 [2, 2, 1024, 768], P('section', None, 'expert', 'head'), may hold values from -6 to 6
- norm_gain: float32 [2, 768], P('section'), may hold values from 0.25 to 1.75
- gate_prob: float32 [2, 2, 1024], P('section', None, 'expert'), may hold values from 0.25 to 1
- expert_ids: int32 [2, 2, 1024], P('section', None, 'expert'), may hold values from 0 to 7, as said below
- slot_ids: int32 [2, 2, 1024], P('section', None, 'expert'), may hold values from 0 to 32, as said below
- weight_in: bfloat16 [2, 8, 768, 3072], P('section', 'expert', None, 'head'), may hold values from -0.21875 to 0.21875
- weight_out: bfloat16 [2, 8, 3072, 768], P('section', 'expert', 'head'), may hold values from -0.109375 to 0.109375
Outputs:
- boundary_out: bfloat16 [2, 2, 1024, 768], P('section', None, 'expert', 'head')
- grad_in: bfloat16 [2, 8, 768, 3072], P('section', 'expert', None, 'head')
- grad_out: bfloat16 [2, 8, 3072, 768], P('section', 'expert', 'head')
The draws below stay inside these ranges and needn't reach their ends.
Inputs may be any that keep to these rules, and one draw needn't show every extreme that they name: `expert_ids`: within each layer and micro-batch, tokens are taken in blocks of 128 (the tokens of one index of expert); in every block one expert, the same for all blocks of that layer and micro-batch, is named by more than 32 tokens. `slot_ids`: A token's slot is the number of earlier tokens of its block that name the same expert, capped at 32; 32 means the token is dropped. So at most 32 tokens of a block hold a slot below 32 at one expert, and in every layer and micro-batch one expert has all 32 slots filled from every block.
All inputs are finite; a program needn't handle non-finite values.
Results may differ from the reference program's by a relative error of at most 0.008.
Values may be sent and summed in bfloat16 or wider, within the bound.
A program may use at most 128 MiB of HBM per device.

```python
import jax
import jax.numpy as jnp
from jax import lax

D = 768
FF = 3072
TOK_DEV = 128
MICRO = 2
EXPERTS = 8
TOKENS = 1024
CAP = 32


def routing(key):
    block_count = TOKENS // TOK_DEV
    streams = jax.random.split(jax.random.fold_in(key, 11), 3)
    favored = jax.random.randint(streams[0], (2, MICRO, 1, 1), 0, EXPERTS)
    random_ids = jax.random.randint(streams[1], (2, MICRO, block_count, TOK_DEV), 0, EXPERTS)
    position = jnp.arange(TOK_DEV, dtype=jnp.int32)
    chosen = jnp.where(position < CAP + 1, favored, random_ids)
    shuffle_score = jax.random.randint(streams[2], (2, MICRO, block_count, TOK_DEV), 0, 2 ** 18) * 4096 + position
    shuffle = jnp.argsort(shuffle_score, axis=-1)
    route_ids = jnp.take_along_axis(chosen, shuffle, axis=-1)
    onehot = (route_ids[..., None] == jnp.arange(EXPERTS, dtype=jnp.int32)).astype(jnp.int32)
    earlier = jnp.sum((jnp.cumsum(onehot, axis=-2) - onehot) * onehot, axis=-1)
    slot_rank = jnp.minimum(earlier, CAP)
    return (route_ids.reshape(2, MICRO, TOKENS).astype(jnp.int32), slot_rank.reshape(2, MICRO, TOKENS).astype(jnp.int32))


def draw_expert_ids(key, part):
    return routing(key)[0]


def draw_slot_ids(key, part):
    return routing(key)[1]


def shard_levels(key, dims, shards, smallest, largest):
    def one(dim, shards_of):
        heights = jax.random.uniform(jax.random.fold_in(jax.random.fold_in(key, 6), dim), (shards_of,), jnp.float32, smallest / len(shards), largest / len(shards))
        return jnp.repeat(jnp.exp(heights), dims[dim] // shards_of).reshape((-1,) + (1,) * (len(dims) - dim - 1))

    factor_of = one(*shards[0])
    for cut in shards[1:]:
        factor_of = factor_of * one(*cut)
    return factor_of


def noise(own_key, extent, deviation, limit, cuts=(), kind=jnp.bfloat16):
    array = deviation * jax.random.normal(own_key, extent, jnp.float32)
    if cuts:
        array = array * shard_levels(own_key, extent, cuts, -0.22, 0.18)
    return jnp.clip(array, -limit, limit).astype(kind)


def setup_inputs(seed: int = 0) -> dict:
    seeds = jax.random.split(jax.random.key(seed), 8)
    boundary = noise(seeds[0], (2, MICRO, TOKENS, D), 1.0, 6.0, ((0, 2), (2, 8), (3, 2)))
    norm_gain = jnp.clip(1.0 + 0.15 * jax.random.normal(seeds[1], (2, D), jnp.float32), 0.25, 1.75)
    gate_prob = jnp.clip(0.25 + 0.75 * jax.random.uniform(seeds[2], (2, MICRO, TOKENS), jnp.float32) ** shard_levels(seeds[2], (2, MICRO, TOKENS), ((0, 2), (2, 8)), -0.2, 0.2), 0.25, 1.0)
    expert_ids = draw_expert_ids(jax.random.fold_in(seeds[7], 71), 0)
    slot_ids = draw_slot_ids(jax.random.fold_in(seeds[7], 71), 0)
    weight_in = noise(seeds[5], (2, EXPERTS, D, FF), D ** -0.5, 0.21875, ((0, 2), (1, 8), (3, 2)))
    weight_out = noise(seeds[6], (2, EXPERTS, FF, D), FF ** -0.5, 0.109375, ((0, 2), (1, 8), (2, 2)))
    return {"boundary": boundary, "norm_gain": norm_gain, "gate_prob": gate_prob, "expert_ids": expert_ids, "slot_ids": slot_ids, "weight_in": weight_in, "weight_out": weight_out}


EPSILON = 1e-06
ROOT_COEF = 0.7978845608
CUBE_COEF = 0.044715

def activate(pre_act):
    tangent = jnp.tanh(ROOT_COEF * (pre_act + CUBE_COEF * pre_act * pre_act * pre_act))
    act_value = 0.5 * pre_act * (1.0 + tangent)
    act_slope = 0.5 * (1.0 + tangent) + 0.5 * pre_act * (1.0 - tangent * tangent) * ROOT_COEF * (1.0 + 3.0 * CUBE_COEF * pre_act * pre_act)
    return (act_value, act_slope)

def rounded(values):
    return lax.optimization_barrier(values.astype(jnp.bfloat16)).astype(jnp.float32)

def placement_rows(slot_ids):
    block_of = jnp.arange(TOKENS, dtype=jnp.int32) // TOK_DEV
    kept_mask = slot_ids < CAP
    row_of = jnp.where(kept_mask, block_of * CAP + slot_ids, TOKENS // TOK_DEV * CAP).astype(jnp.int32)
    return (kept_mask, row_of)

def dispatch(tokens, expert_ids, row_of):
    buffer = jnp.zeros((EXPERTS, TOKENS // TOK_DEV * CAP, D), tokens.dtype)
    return buffer.at[expert_ids, row_of].set(tokens, mode='drop')

def collect(buffer, expert_ids, row_of, kept_mask):
    last_row = buffer.shape[1] - 1
    picked = buffer[expert_ids, jnp.minimum(row_of, last_row)]
    return jnp.where(kept_mask[:, None], picked.astype(jnp.float32), jnp.float32(0.0))

def normalize(rows_in, gain):
    values = rows_in.astype(jnp.float32)
    inv_scale = lax.rsqrt(lax.optimization_barrier(jnp.mean(values * values, axis=-1, keepdims=True)) + EPSILON)
    return (values * inv_scale * gain).astype(jnp.bfloat16)

def layer_forward(tokens, gain, weight_in, weight_out, expert_ids, slot_ids, gate_prob):
    kept_mask, row_of = placement_rows(slot_ids)
    buffer = dispatch(tokens, expert_ids, row_of)
    half_ff = FF // 2

    def per_expert(operands):
        rows_in, first_weight, second_weight = operands
        normed = normalize(rows_in, gain)
        pre_act = jnp.dot(normed, first_weight, preferred_element_type=jnp.float32)
        act_value = activate(pre_act)[0].astype(jnp.bfloat16)
        part_low = jnp.dot(act_value[:, :half_ff], second_weight[:half_ff], preferred_element_type=jnp.float32)
        part_high = jnp.dot(act_value[:, half_ff:], second_weight[half_ff:], preferred_element_type=jnp.float32)
        return (rounded(part_low) + rounded(part_high)).astype(jnp.bfloat16)
    outputs = lax.map(per_expert, (buffer, weight_in, weight_out))
    combined = collect(outputs, expert_ids, row_of, kept_mask)
    return (tokens.astype(jnp.float32) + gate_prob[:, None] * combined).astype(jnp.bfloat16)

def layer_backward(tokens, grad_tok, gain, weight_in, weight_out, expert_ids, slot_ids, gate_prob):
    kept_mask, row_of = placement_rows(slot_ids)
    buffer = dispatch(tokens, expert_ids, row_of)
    sent_grad = (gate_prob[:, None] * grad_tok.astype(jnp.float32)).astype(jnp.bfloat16)
    grad_buffer = dispatch(sent_grad, expert_ids, row_of)
    half_ff = FF // 2

    def per_expert(operands):
        rows_in, grad_rows, first_weight, second_weight = operands
        normed = normalize(rows_in, gain)
        pre_act = jnp.dot(normed, first_weight, preferred_element_type=jnp.float32)
        act_slope = activate(pre_act)[1]
        grad_act = jnp.dot(grad_rows, second_weight.T, preferred_element_type=jnp.float32)
        grad_pre = (grad_act * act_slope).astype(jnp.bfloat16)
        part_low = jnp.dot(grad_pre[:, :half_ff], first_weight[:, :half_ff].T, preferred_element_type=jnp.float32)
        part_high = jnp.dot(grad_pre[:, half_ff:], first_weight[:, half_ff:].T, preferred_element_type=jnp.float32)
        return (rounded(part_low) + rounded(part_high)).astype(jnp.bfloat16)
    grad_normed = lax.map(per_expert, (buffer, grad_buffer, weight_in, weight_out))
    grad_back = collect(grad_normed, expert_ids, row_of, kept_mask)
    values = tokens.astype(jnp.float32)
    inv_scale = lax.rsqrt(lax.optimization_barrier(jnp.mean(values * values, axis=-1, keepdims=True)) + EPSILON)
    scaled_grad = gain * grad_back
    cross_sum = lax.optimization_barrier(jnp.sum(scaled_grad * values, axis=-1, keepdims=True))
    result = grad_tok.astype(jnp.float32) + inv_scale * scaled_grad - values * inv_scale * inv_scale * inv_scale * cross_sum / D
    return result.astype(jnp.bfloat16)

def layer_gradients(inputs, cotangents, gain, weight_in, weight_out, expert_ids, slot_ids, gate_prob):
    row_buffers = []
    grad_buffers = []
    for micro_index in range(MICRO):
        kept_mask, row_of = placement_rows(slot_ids[micro_index])
        row_buffers.append(dispatch(inputs[micro_index], expert_ids[micro_index], row_of))
        sent_grad = (gate_prob[micro_index][:, None] * cotangents[micro_index].astype(jnp.float32)).astype(jnp.bfloat16)
        grad_buffers.append(dispatch(sent_grad, expert_ids[micro_index], row_of))
    rows_all = jnp.stack(row_buffers, axis=1)
    grads_all = jnp.stack(grad_buffers, axis=1)

    def per_expert(operands):
        rows_each, grads_each, first_weight, second_weight = operands
        total_in = jnp.zeros((D, FF), jnp.float32)
        total_out = jnp.zeros((FF, D), jnp.float32)
        for micro_index in range(MICRO):
            normed = normalize(rows_each[micro_index], gain)
            pre_act = jnp.dot(normed, first_weight, preferred_element_type=jnp.float32)
            act_value, act_slope = activate(pre_act)
            grad_act = jnp.dot(grads_each[micro_index], second_weight.T, preferred_element_type=jnp.float32)
            grad_pre = (grad_act * act_slope).astype(jnp.bfloat16)
            total_in = total_in + jnp.dot(normed.T, grad_pre, preferred_element_type=jnp.float32)
            total_out = total_out + jnp.dot(act_value.astype(jnp.bfloat16).T, grads_each[micro_index], preferred_element_type=jnp.float32)
        return (total_in.astype(jnp.bfloat16), total_out.astype(jnp.bfloat16))
    return lax.map(per_expert, (rows_all, grads_all, weight_in, weight_out))

def reference(boundary, norm_gain, gate_prob, expert_ids, slot_ids, weight_in, weight_out):
    hiddens = []
    tops = []
    grad_hiddens = []
    bottoms = []
    for micro_index in range(MICRO):
        hidden = layer_forward(boundary[0, micro_index], norm_gain[0], weight_in[0], weight_out[0], expert_ids[0, micro_index], slot_ids[0, micro_index], gate_prob[0, micro_index])
        top_out = layer_forward(hidden, norm_gain[1], weight_in[1], weight_out[1], expert_ids[1, micro_index], slot_ids[1, micro_index], gate_prob[1, micro_index])
        grad_hidden = layer_backward(hidden, boundary[1, micro_index], norm_gain[1], weight_in[1], weight_out[1], expert_ids[1, micro_index], slot_ids[1, micro_index], gate_prob[1, micro_index])
        bottom = layer_backward(boundary[0, micro_index], grad_hidden, norm_gain[0], weight_in[0], weight_out[0], expert_ids[0, micro_index], slot_ids[0, micro_index], gate_prob[0, micro_index])
        hiddens.append(hidden)
        tops.append(top_out)
        grad_hiddens.append(grad_hidden)
        bottoms.append(bottom)
    boundary_out = jnp.stack([jnp.stack(bottoms), jnp.stack(tops)])
    lower_in, lower_out = layer_gradients(boundary[0], jnp.stack(grad_hiddens), norm_gain[0], weight_in[0], weight_out[0], expert_ids[0], slot_ids[0], gate_prob[0])
    upper_in, upper_out = layer_gradients(jnp.stack(hiddens), boundary[1], norm_gain[1], weight_in[1], weight_out[1], expert_ids[1], slot_ids[1], gate_prob[1])
    return (boundary_out, jnp.stack([lower_in, upper_in]), jnp.stack([lower_out, upper_out]))
```

```python
import functools

import jax
import jax.numpy as jnp
from jax import lax
from jax.experimental import pallas as pl
from jax.experimental.pallas import tpu as pltpu
from jax.sharding import PartitionSpec as P

EPSILON = 1e-06
ROOT_COEF = 0.7978845608
CUBE_COEF = 0.044715
MESH = pl.DeviceIdType.MESH
BF16 = jnp.bfloat16
F32 = jnp.float32
FWD, BWD = 0, 1
SQUARE, CROSS = 0, 1
COLS = 256


def activate(pre_act):
    tangent = jnp.tanh(ROOT_COEF * (pre_act + CUBE_COEF * pre_act * pre_act * pre_act))
    act_value = 0.5 * pre_act * (1.0 + tangent)
    act_slope = 0.5 * (1.0 + tangent) + 0.5 * pre_act * (1.0 - tangent * tangent) * ROOT_COEF * (
        1.0 + 3.0 * CUBE_COEF * pre_act * pre_act
    )
    return (act_value, act_slope)


def dot(left, right, dims=((1,), (0,))):
    return lax.dot_general(left, right, (dims, ((), ())), preferred_element_type=F32)


NT = ((1,), (1,))
TN = ((0,), (0,))


def kernel(
    experts, cap, pad,
    local_ref, gain_ref, prob_ref, ids_ref, slots_ref, win_ref, wout_ref,
    out_ref, gin_ref, gout_ref,
    tab, send, rows, normed, act, gpre, mid, keep, away, recvp, back, sec_src, sec_in, xsend, xrecv,
    s1, r1, s2, r2, s3, r3, s4, r4, s5, r5, s6, r6,
):
    sec, me, head = lax.axis_index("section"), lax.axis_index("expert"), lax.axis_index("head")
    other = 1 - head
    micro, tok, half = local_ref.shape
    full = 2 * half
    total = experts * pad
    hidden_half = win_ref.shape[1]
    chunks = hidden_half // COLS
    own_cols = pl.ds(pl.multiple_of(head * half, 128), half)
    other_cols = pl.ds(pl.multiple_of(other * half, 128), half)

    barrier = pltpu.get_barrier_semaphore()

    def each_peer(action):
        def step(k, carry):
            action(lax.rem(me + k, experts))
            return carry

        lax.fori_loop(1, experts, step, 0)

    each_peer(
        lambda d: pl.semaphore_signal(barrier, inc=1, device_id={"expert": d}, device_id_type=MESH)
    )
    pl.semaphore_signal(barrier, inc=1, device_id={"head": other}, device_id_type=MESH)
    pl.semaphore_signal(barrier, inc=1, device_id={"section": 1 - sec}, device_id_type=MESH)

    def slot_rows(index):
        return pl.ds(pl.multiple_of(index * pad, pad), pad)

    def micro_rows(m, index):
        return pl.ds(pl.multiple_of(m * total + index * pad, pad), pad)

    def span(m):
        return slice(m * total, (m + 1) * total)

    eye = lax.broadcasted_iota(jnp.int32, (tok, tok), 0) == lax.broadcasted_iota(
        jnp.int32, (tok, tok), 1
    )

    def to_col(row):
        return jnp.sum(jnp.where(eye, row, 0.0), axis=1, keepdims=True)

    def to_row(col):
        return jnp.sum(jnp.where(eye, col, 0.0), axis=0, keepdims=True)

    for m in range(micro):
        ids, slots = ids_ref[m : m + 1, :], slots_ref[m : m + 1, :]
        target = jnp.where(slots < cap, ids * pad + slots, -1)
        hit = target == lax.broadcasted_iota(jnp.int32, (total, tok), 0)
        tab[m] = jnp.where(hit, 1.0, 0.0).astype(BF16)
    prob = [to_col(prob_ref[m : m + 1, :]) for m in range(micro)]
    gain = gain_ref[...]
    gain_half = gain_ref[:, own_cols]

    def chunk_copy(kind, m, dst, came_from):
        return pltpu.make_async_remote_copy(
            src_ref=send.at[kind, m, slot_rows(dst), :],
            dst_ref=rows.at[kind, micro_rows(m, came_from), own_cols],
            send_sem=s1.at[kind, m, dst],
            recv_sem=r1.at[kind, m, came_from],
            device_id={"expert": dst},
            device_id_type=MESH,
        )

    def relay_copy(kind, m, block, cols):
        return pltpu.make_async_remote_copy(
            src_ref=rows.at[kind, micro_rows(m, block), own_cols],
            dst_ref=rows.at[kind, micro_rows(m, block), cols],
            send_sem=s2.at[kind, m, block],
            recv_sem=r2.at[kind, m, block],
            device_id={"head": other},
            device_id_type=MESH,
        )

    def place(kind, m, tokens):
        send[kind, m] = dot(tab[m], tokens).astype(BF16)

    def dispatch(kind, m):
        each_peer(lambda d: chunk_copy(kind, m, d, me).start())
        rows[kind, micro_rows(m, me), own_cols] = send[kind, m, slot_rows(me), :]
        relay_copy(kind, m, me, own_cols).start()

    def relay(kind, m):
        def one(block):
            chunk_copy(kind, m, block, block).wait_recv()
            relay_copy(kind, m, block, own_cols).start()

        each_peer(one)

    def arrived(kind, m):
        relay_copy(kind, m, me, other_cols).wait_recv()
        each_peer(lambda block: relay_copy(kind, m, block, other_cols).wait_recv())

    def away_copy(kind, m):
        return pltpu.make_async_remote_copy(
            src_ref=away.at[kind, m],
            dst_ref=recvp.at[kind, m],
            send_sem=s3.at[kind, m],
            recv_sem=r3.at[kind, m],
            device_id={"head": other},
            device_id_type=MESH,
        )

    def back_copy(kind, m, dst, came_from):
        return pltpu.make_async_remote_copy(
            src_ref=keep.at[kind, m, slot_rows(dst), :],
            dst_ref=back.at[kind, m, slot_rows(came_from), :],
            send_sem=s4.at[kind, m, dst],
            recv_sem=r4.at[kind, m, came_from],
            device_id={"expert": dst},
            device_id_type=MESH,
        )

    def send_back(kind, m):
        away_copy(kind, m).wait_recv()
        summed = keep[kind, m].astype(F32) + recvp[kind, m].astype(F32)
        keep[kind, m] = summed.astype(BF16)
        each_peer(lambda d: back_copy(kind, m, d, me).start())
        back[kind, m, slot_rows(me), :] = keep[kind, m, slot_rows(me), :]

    def collect(kind, m):
        each_peer(lambda block: back_copy(kind, m, block, block).wait_recv())
        return dot(tab[m], back[kind, m], TN)

    def section_copy(m):
        return pltpu.make_async_remote_copy(
            src_ref=sec_src.at[m],
            dst_ref=sec_in.at[m],
            send_sem=s5.at[m],
            recv_sem=r5.at[m],
            device_id={"section": 1 - sec},
            device_id_type=MESH,
        )

    def sum_copy(what, m):
        return pltpu.make_async_remote_copy(
            src_ref=xsend.at[what, m],
            dst_ref=xrecv.at[what, m],
            send_sem=s6.at[what, m],
            recv_sem=r6.at[what, m],
            device_id={"head": other},
            device_id_type=MESH,
        )

    def sum_start(what, m, col):
        xsend[what, m] = jnp.broadcast_to(to_row(col), (8, tok))
        sum_copy(what, m).start()

    def sum_done(what, m):
        sum_copy(what, m).wait_recv()
        return to_col(xsend[what, m, 0:1, :] + xrecv[what, m, 0:1, :])

    def square_start(m, tokens):
        values = tokens.astype(F32)
        sum_start(SQUARE, m, jnp.sum(values * values, axis=1, keepdims=True))

    def normalize(m):
        values = rows[FWD, span(m), :].astype(F32)
        inv_scale = lax.rsqrt(jnp.mean(values * values, axis=-1, keepdims=True) + EPSILON)
        normed[span(m), :] = (values * inv_scale * gain).astype(BF16)

    def each_chunk(action):
        def step(c, carry):
            action(pl.ds(pl.multiple_of(c * COLS, COLS), COLS))
            return carry

        lax.fori_loop(0, chunks, step, 0)

    def out_partial(m):
        away[FWD, m] = dot(act[span(m), :], wout_ref[:, other_cols]).astype(BF16)
        away_copy(FWD, m).start()
        keep[FWD, m] = dot(act[span(m), :], wout_ref[:, own_cols]).astype(BF16)

    def grad_partial(m):
        away[BWD, m] = dot(gpre[span(m), :], win_ref[other_cols, :], NT).astype(BF16)
        away_copy(BWD, m).start()
        keep[BWD, m] = dot(gpre[span(m), :], win_ref[own_cols, :], NT).astype(BF16)

    def layer_out(m, tokens):
        return (tokens.astype(F32) + prob[m] * collect(FWD, m)).astype(BF16)

    def sent_grad(m, cot):
        return (prob[m] * cot.astype(F32)).astype(BF16)

    def cross_start(m, tokens):
        scaled = gain_half * collect(BWD, m)
        sum_start(CROSS, m, jnp.sum(scaled * tokens.astype(F32), axis=1, keepdims=True))
        return scaled

    def layer_grad(m, tokens, cot, scaled):
        inv = lax.rsqrt(sum_done(SQUARE, m) / full + EPSILON)
        cross = sum_done(CROSS, m)
        values = tokens.astype(F32)
        return (
            cot.astype(F32) + inv * scaled - values * (inv * inv * inv * cross / full)
        ).astype(BF16)

    def weight_grads():
        def first(c, carry):
            part = pl.ds(pl.multiple_of(c * COLS, COLS), COLS)
            gin_ref[part, :] = dot(normed[:, part], gpre[...], TN).astype(BF16)
            return carry

        lax.fori_loop(0, full // COLS, first, 0)

        def second(part):
            gout_ref[part, :] = dot(act[:, part], rows[BWD], TN).astype(BF16)

        each_chunk(second)


    @pl.when(sec == 0)
    def _():
        for m in range(micro):
            place(FWD, m, local_ref[m])
        pl.semaphore_wait(barrier, experts + 1)
        for m in range(micro):
            dispatch(FWD, m)
        for m in range(micro):
            square_start(m, local_ref[m])

        def forward(m):
            arrived(FWD, m)
            normalize(m)

            def chunk(part):
                pre = dot(normed[span(m), :], win_ref[:, part])
                value, slope = activate(pre)
                act[span(m), part] = value.astype(BF16)
                mid[span(m), part] = slope.astype(mid.dtype)

            each_chunk(chunk)
            out_partial(m)

        def hidden(m):
            sec_src[m] = layer_out(m, local_ref[m])
            section_copy(m).start()

        relay(FWD, 0)
        forward(0)
        relay(FWD, 1)
        send_back(FWD, 0)
        forward(1)
        hidden(0)
        send_back(FWD, 1)
        hidden(1)

        def grad_in(m):
            section_copy(m).wait_recv()
            place(BWD, m, sent_grad(m, sec_in[m]))
            dispatch(BWD, m)

        def backward(m):
            arrived(BWD, m)

            def chunk(part):
                grad_act = dot(rows[BWD, span(m), :], wout_ref[part, :], NT)
                gpre[span(m), part] = (grad_act * mid[span(m), part].astype(F32)).astype(BF16)

            each_chunk(chunk)
            grad_partial(m)

        grad_in(0)
        relay(BWD, 0)
        backward(0)
        grad_in(1)
        send_back(BWD, 0)
        relay(BWD, 1)
        backward(1)
        scaled0 = cross_start(0, local_ref[0])
        send_back(BWD, 1)
        out_ref[0] = layer_grad(0, local_ref[0], sec_in[0], scaled0)
        weight_grads()
        scaled1 = cross_start(1, local_ref[1])
        out_ref[1] = layer_grad(1, local_ref[1], sec_in[1], scaled1)

    @pl.when(sec != 0)
    def _():
        for m in range(micro):
            place(BWD, m, sent_grad(m, local_ref[m]))
        pl.semaphore_wait(barrier, experts + 1)
        for m in range(micro):
            dispatch(BWD, m)
        for m in range(micro):
            relay(BWD, m)
        for m in range(micro):
            arrived(BWD, m)

            def early(part):
                grad_act = dot(rows[BWD, span(m), :], wout_ref[part, :], NT)
                mid[span(m), part] = grad_act.astype(mid.dtype)

            each_chunk(early)

        def hidden_in(m):
            section_copy(m).wait_recv()
            place(FWD, m, sec_in[m])
            dispatch(FWD, m)
            square_start(m, sec_in[m])

        def both(m):
            arrived(FWD, m)
            normalize(m)

            def chunk(part):
                pre = dot(normed[span(m), :], win_ref[:, part])
                value, slope = activate(pre)
                act[span(m), part] = value.astype(BF16)
                gpre[span(m), part] = (mid[span(m), part].astype(F32) * slope).astype(BF16)

            each_chunk(chunk)
            grad_partial(m)

        def finish(m, scaled):
            sec_src[m] = layer_grad(m, sec_in[m], local_ref[m], scaled)
            section_copy(m).start()

        hidden_in(0)
        relay(FWD, 0)
        both(0)
        hidden_in(1)
        send_back(BWD, 0)
        relay(FWD, 1)
        both(1)
        scaled0 = cross_start(0, sec_in[0])
        send_back(BWD, 1)
        finish(0, scaled0)
        out_partial(0)
        scaled1 = cross_start(1, sec_in[1])
        send_back(FWD, 0)
        finish(1, scaled1)
        out_partial(1)
        send_back(FWD, 1)
        weight_grads()
        for m in range(micro):
            out_ref[m] = layer_out(m, sec_in[m])

    for m in range(micro):
        for kind in (FWD, BWD):
            def drain(block):
                chunk_copy(kind, m, block, me).wait_send()
                relay_copy(kind, m, block, own_cols).wait_send()
                back_copy(kind, m, block, me).wait_send()

            each_peer(drain)
            relay_copy(kind, m, me, own_cols).wait_send()
            away_copy(kind, m).wait_send()
        section_copy(m).wait_send()
        sum_copy(SQUARE, m).wait_send()
        sum_copy(CROSS, m).wait_send()


def on_device(boundary, norm_gain, gate_prob, expert_ids, slot_ids, weight_in, weight_out):
    experts = lax.axis_size("expert")
    micro, tok, half = boundary.shape[1:]
    full, hidden_half = weight_in.shape[2:]
    cap = 2 * tok // experts
    pad = -(-cap // 16) * 16
    total = experts * pad
    mid_type = F32 if total <= 512 else BF16
    vmem = pl.BlockSpec(memory_space=pltpu.VMEM)
    per_block = pltpu.SemaphoreType.DMA((2, micro, experts))
    per_pair = pltpu.SemaphoreType.DMA((2, micro))
    per_micro = pltpu.SemaphoreType.DMA((micro,))
    pieces = pltpu.VMEM((2, micro, total, half), BF16)
    tokens = pltpu.VMEM((micro, tok, half), BF16)
    sums = pltpu.VMEM((2, micro, 8, tok), F32)
    out, grad_in, grad_out = pl.pallas_call(
        functools.partial(kernel, experts, cap, pad),
        out_shape=(
            jax.ShapeDtypeStruct((micro, tok, half), BF16),
            jax.ShapeDtypeStruct((full, hidden_half), BF16),
            jax.ShapeDtypeStruct((hidden_half, full), BF16),
        ),
        in_specs=[vmem] * 7,
        out_specs=(vmem, vmem, vmem),
        scratch_shapes=[
            pltpu.VMEM((micro, total, tok), BF16),
            pieces,
            pltpu.VMEM((2, micro * total, full), BF16),
            pltpu.VMEM((micro * total, full), BF16),
            pltpu.VMEM((micro * total, hidden_half), BF16),
            pltpu.VMEM((micro * total, hidden_half), BF16),
            pltpu.VMEM((micro * total, hidden_half), mid_type),
            pieces,
            pieces,
            pieces,
            pieces,
            tokens,
            tokens,
            sums,
            sums,
            per_block, per_block,
            per_block, per_block,
            per_pair, per_pair,
            per_block, per_block,
            per_micro, per_micro,
            per_pair, per_pair,
        ],
        compiler_params=pltpu.CompilerParams(collective_id=0, has_side_effects=True),
    )(
        boundary[0], norm_gain, gate_prob[0], expert_ids[0], slot_ids[0],
        weight_in[0, 0], weight_out[0, 0],
    )
    return (out[None], grad_in[None, None], grad_out[None, None])


def solution(mesh):
    placed = (
        P("section", None, "expert", "head"),
        P("section", None),
        P("section", None, "expert"),
        P("section", None, "expert"),
        P("section", None, "expert"),
        P("section", "expert", None, "head"),
        P("section", "expert", "head", None),
    )
    return jax.shard_map(
        on_device,
        mesh=mesh,
        in_specs=placed,
        out_specs=(
            P("section", None, "expert", "head"),
            P("section", "expert", None, "head"),
            P("section", "expert", "head", None),
        ),
        check_vma=False,
    )
```

```python
import functools

import jax
import jax.numpy as jnp
from jax import lax
from jax.experimental import pallas as pl
from jax.experimental.pallas import tpu as pltpu
from jax.sharding import PartitionSpec as P

EPSILON = 1e-06
ROOT_COEF = 0.7978845608
CUBE_COEF = 0.044715
MESH = pl.DeviceIdType.MESH
BF16 = jnp.bfloat16
F32 = jnp.float32
FWD, BWD = 0, 1
SQUARE, CROSS = 0, 1
COLS = 256
SPLIT = 2
VMEM_LIMIT = 56 * 2**20
COPY_LIMIT = 2**20


def activate(pre_act):
    tangent = jnp.tanh(ROOT_COEF * (pre_act + CUBE_COEF * pre_act * pre_act * pre_act))
    act_value = 0.5 * pre_act * (1.0 + tangent)
    act_slope = 0.5 * (1.0 + tangent) + 0.5 * pre_act * (1.0 - tangent * tangent) * ROOT_COEF * (
        1.0 + 3.0 * CUBE_COEF * pre_act * pre_act
    )
    return (act_value, act_slope)


def dot(left, right, dims=((1,), (0,))):
    return lax.dot_general(left, right, (dims, ((), ())), preferred_element_type=F32)


NT = ((1,), (1,))
TN = ((0,), (0,))


def kernel(
    experts, cap, pad,
    local_ref, gain_ref, prob_ref, ids_ref, slots_ref, win_hbm, wout_hbm,
    out_ref, gin_ref, gout_ref,
    tab, send, rows, normed, act, gpre, mid, keep, away, recvp, back, sec_src, sec_in, xsend, xrecv,
    win_ref, wout_ref, load_sem,
    s1, r1, s2, r2, s3, r3, s4, r4, s5, r5, s6, r6,
):
    win_load = pltpu.make_async_copy(win_hbm, win_ref, load_sem.at[0])
    wout_load = pltpu.make_async_copy(wout_hbm, wout_ref, load_sem.at[1])
    win_load.start()
    wout_load.start()
    sec, me, head = lax.axis_index("section"), lax.axis_index("expert"), lax.axis_index("head")
    other = 1 - head
    micro, tok, half = local_ref.shape
    full = 2 * half
    total = experts * pad
    hidden_half = win_ref.shape[1]
    chunks = hidden_half // COLS
    own_cols = pl.ds(pl.multiple_of(head * half, 128), half)
    other_cols = pl.ds(pl.multiple_of(other * half, 128), half)

    barrier = pltpu.get_barrier_semaphore()

    def each_peer(action):
        def step(k, carry):
            action(lax.rem(me + k, experts))
            return carry

        lax.fori_loop(1, experts, step, 0)

    def greet(d):
        for h in range(2):
            pl.semaphore_signal(
                barrier, inc=1, device_id={"expert": d, "head": h}, device_id_type=MESH
            )

    each_peer(greet)
    pl.semaphore_signal(barrier, inc=1, device_id={"head": other}, device_id_type=MESH)
    pl.semaphore_signal(barrier, inc=1, device_id={"section": 1 - sec}, device_id_type=MESH)

    def slot_rows(index):
        return pl.ds(pl.multiple_of(index * pad, pad), pad)

    def micro_rows(m, index):
        return pl.ds(pl.multiple_of(m * total + index * pad, pad), pad)

    def span(m):
        return slice(m * total, (m + 1) * total)

    eye = lax.broadcasted_iota(jnp.int32, (tok, tok), 0) == lax.broadcasted_iota(
        jnp.int32, (tok, tok), 1
    )

    def to_col(row):
        return jnp.sum(jnp.where(eye, row, 0.0), axis=1, keepdims=True)

    def to_row(col):
        return jnp.sum(jnp.where(eye, col, 0.0), axis=0, keepdims=True)

    for m in range(micro):
        ids, slots = ids_ref[m : m + 1, :], slots_ref[m : m + 1, :]
        target = jnp.where(slots < cap, ids * pad + slots, -1)
        hit = target == lax.broadcasted_iota(jnp.int32, (total, tok), 0)
        tab[m] = jnp.where(hit, 1.0, 0.0).astype(BF16)
    prob = [to_col(prob_ref[m : m + 1, :]) for m in range(micro)]
    gain = gain_ref[...]
    gain_half = gain_ref[:, own_cols]

    def chunk_copy(kind, m, dst, came_from):
        return pltpu.make_async_remote_copy(
            src_ref=send.at[kind, m, slot_rows(dst), :],
            dst_ref=rows.at[kind, micro_rows(m, came_from), own_cols],
            send_sem=s1.at[kind, m, dst],
            recv_sem=r1.at[kind, m, came_from],
            device_id={"expert": dst},
            device_id_type=MESH,
        )

    def cross_copy(kind, m, dst, came_from, cols):
        return pltpu.make_async_remote_copy(
            src_ref=send.at[kind, m, slot_rows(dst), :],
            dst_ref=rows.at[kind, micro_rows(m, came_from), cols],
            send_sem=s2.at[kind, m, dst],
            recv_sem=r2.at[kind, m, came_from],
            device_id={"expert": dst, "head": other},
            device_id_type=MESH,
        )

    def place(kind, m, tokens):
        send[kind, m] = dot(tab[m], tokens).astype(BF16)

    def dispatch(kind, m):
        def both_heads(d):
            cross_copy(kind, m, d, me, own_cols).start()
            chunk_copy(kind, m, d, me).start()

        each_peer(both_heads)
        cross_copy(kind, m, me, me, own_cols).start()
        rows[kind, micro_rows(m, me), own_cols] = send[kind, m, slot_rows(me), :]

    def arrived(kind, m):
        def both_heads(block):
            chunk_copy(kind, m, block, block).wait_recv()
            cross_copy(kind, m, block, block, other_cols).wait_recv()

        cross_copy(kind, m, me, me, other_cols).wait_recv()
        each_peer(both_heads)

    def piece(c):
        return slice(c * (total // SPLIT), (c + 1) * (total // SPLIT))

    def piece_of(m, c):
        return slice(m * total + c * (total // SPLIT), m * total + (c + 1) * (total // SPLIT))

    def away_copy(kind, m, c):
        return pltpu.make_async_remote_copy(
            src_ref=away.at[kind, m, piece(c), :],
            dst_ref=recvp.at[kind, m, piece(c), :],
            send_sem=s3.at[kind, m, c],
            recv_sem=r3.at[kind, m, c],
            device_id={"head": other},
            device_id_type=MESH,
        )

    def back_copy(kind, m, dst, came_from):
        return pltpu.make_async_remote_copy(
            src_ref=keep.at[kind, m, slot_rows(dst), :],
            dst_ref=back.at[kind, m, slot_rows(came_from), :],
            send_sem=s4.at[kind, m, dst],
            recv_sem=r4.at[kind, m, came_from],
            device_id={"expert": dst},
            device_id_type=MESH,
        )

    def send_back(kind, m):
        for c in range(SPLIT):
            away_copy(kind, m, c).wait_recv()
            summed = keep[kind, m, piece(c), :].astype(F32) + recvp[kind, m, piece(c), :].astype(F32)
            keep[kind, m, piece(c), :] = summed.astype(BF16)

            def one(dst, carry):
                @pl.when(dst != me)
                def _():
                    back_copy(kind, m, dst, me).start()

                return carry

            lax.fori_loop(c * experts // SPLIT, (c + 1) * experts // SPLIT, one, 0)
        back[kind, m, slot_rows(me), :] = keep[kind, m, slot_rows(me), :]

    def collect(kind, m):
        each_peer(lambda block: back_copy(kind, m, block, block).wait_recv())
        return dot(tab[m], back[kind, m], TN)

    def section_copy(m):
        return pltpu.make_async_remote_copy(
            src_ref=sec_src.at[m],
            dst_ref=sec_in.at[m],
            send_sem=s5.at[m],
            recv_sem=r5.at[m],
            device_id={"section": 1 - sec},
            device_id_type=MESH,
        )

    def sum_copy(what, m):
        return pltpu.make_async_remote_copy(
            src_ref=xsend.at[what, m],
            dst_ref=xrecv.at[what, m],
            send_sem=s6.at[what, m],
            recv_sem=r6.at[what, m],
            device_id={"head": other},
            device_id_type=MESH,
        )

    def sum_start(what, m, col):
        xsend[what, m] = jnp.broadcast_to(to_row(col), (8, tok))
        sum_copy(what, m).start()

    def sum_done(what, m):
        sum_copy(what, m).wait_recv()
        return to_col(xsend[what, m, 0:1, :] + xrecv[what, m, 0:1, :])

    def square_start(m, tokens):
        values = tokens.astype(F32)
        sum_start(SQUARE, m, jnp.sum(values * values, axis=1, keepdims=True))

    def normalize(m):
        values = rows[FWD, span(m), :].astype(F32)
        inv_scale = lax.rsqrt(jnp.mean(values * values, axis=-1, keepdims=True) + EPSILON)
        normed[span(m), :] = (values * inv_scale * gain).astype(BF16)

    def each_chunk(action):
        def step(c, carry):
            action(pl.ds(pl.multiple_of(c * COLS, COLS), COLS))
            return carry

        lax.fori_loop(0, chunks, step, 0)

    def out_partial(m):
        for c in range(SPLIT):
            away[FWD, m, piece(c), :] = dot(act[piece_of(m, c), :], wout_ref[:, other_cols]).astype(
                BF16
            )
            away_copy(FWD, m, c).start()
        keep[FWD, m] = dot(act[span(m), :], wout_ref[:, own_cols]).astype(BF16)

    def grad_partial(m):
        for c in range(SPLIT):
            away[BWD, m, piece(c), :] = dot(gpre[piece_of(m, c), :], win_ref[other_cols, :], NT).astype(
                BF16
            )
            away_copy(BWD, m, c).start()
        keep[BWD, m] = dot(gpre[span(m), :], win_ref[own_cols, :], NT).astype(BF16)

    def layer_out(m, tokens):
        return (tokens.astype(F32) + prob[m] * collect(FWD, m)).astype(BF16)

    def sent_grad(m, cot):
        return (prob[m] * cot.astype(F32)).astype(BF16)

    def cross_start(m, tokens):
        scaled = gain_half * collect(BWD, m)
        sum_start(CROSS, m, jnp.sum(scaled * tokens.astype(F32), axis=1, keepdims=True))
        return scaled

    def layer_grad(m, tokens, cot, scaled):
        inv = lax.rsqrt(sum_done(SQUARE, m) / full + EPSILON)
        cross = sum_done(CROSS, m)
        values = tokens.astype(F32)
        return (
            cot.astype(F32) + inv * scaled - values * (inv * inv * inv * cross / full)
        ).astype(BF16)

    def weight_grads():
        def first(c, carry):
            part = pl.ds(pl.multiple_of(c * COLS, COLS), COLS)
            gin_ref[part, :] = dot(normed[:, part], gpre[...], TN).astype(BF16)
            return carry

        lax.fori_loop(0, full // COLS, first, 0)

        def second(part):
            gout_ref[part, :] = dot(act[:, part], rows[BWD], TN).astype(BF16)

        each_chunk(second)


    @pl.when(sec == 0)
    def _():
        for m in range(micro):
            place(FWD, m, local_ref[m])
        pl.semaphore_wait(barrier, 2 * experts)
        for m in range(micro):
            dispatch(FWD, m)
        for m in range(micro):
            square_start(m, local_ref[m])
        win_load.wait()
        wout_load.wait()

        def forward(m):
            arrived(FWD, m)
            normalize(m)

            def chunk(part):
                pre = dot(normed[span(m), :], win_ref[:, part])
                value, slope = activate(pre)
                act[span(m), part] = value.astype(BF16)
                mid[span(m), part] = slope.astype(mid.dtype)

            each_chunk(chunk)
            out_partial(m)

        def hidden(m):
            sec_src[m] = layer_out(m, local_ref[m])
            section_copy(m).start()

        forward(0)
        send_back(FWD, 0)
        forward(1)
        hidden(0)
        send_back(FWD, 1)
        hidden(1)

        def grad_in(m):
            section_copy(m).wait_recv()
            place(BWD, m, sent_grad(m, sec_in[m]))
            dispatch(BWD, m)

        def backward(m):
            arrived(BWD, m)

            def chunk(part):
                grad_act = dot(rows[BWD, span(m), :], wout_ref[part, :], NT)
                gpre[span(m), part] = (grad_act * mid[span(m), part].astype(F32)).astype(BF16)

            each_chunk(chunk)
            grad_partial(m)

        grad_in(0)
        backward(0)
        grad_in(1)
        send_back(BWD, 0)
        backward(1)
        scaled0 = cross_start(0, local_ref[0])
        send_back(BWD, 1)
        out_ref[0] = layer_grad(0, local_ref[0], sec_in[0], scaled0)
        weight_grads()
        scaled1 = cross_start(1, local_ref[1])
        out_ref[1] = layer_grad(1, local_ref[1], sec_in[1], scaled1)

    @pl.when(sec != 0)
    def _():
        for m in range(micro):
            place(BWD, m, sent_grad(m, local_ref[m]))
        pl.semaphore_wait(barrier, 2 * experts)
        for m in range(micro):
            dispatch(BWD, m)
        win_load.wait()
        wout_load.wait()
        for m in range(micro):
            arrived(BWD, m)

            def early(part):
                grad_act = dot(rows[BWD, span(m), :], wout_ref[part, :], NT)
                mid[span(m), part] = grad_act.astype(mid.dtype)

            each_chunk(early)

        def hidden_in(m):
            section_copy(m).wait_recv()
            place(FWD, m, sec_in[m])
            dispatch(FWD, m)
            square_start(m, sec_in[m])

        def both(m):
            arrived(FWD, m)
            normalize(m)

            def chunk(part):
                pre = dot(normed[span(m), :], win_ref[:, part])
                value, slope = activate(pre)
                act[span(m), part] = value.astype(BF16)
                gpre[span(m), part] = (mid[span(m), part].astype(F32) * slope).astype(BF16)

            each_chunk(chunk)
            grad_partial(m)

        def finish(m, scaled):
            sec_src[m] = layer_grad(m, sec_in[m], local_ref[m], scaled)
            section_copy(m).start()

        hidden_in(0)
        both(0)
        hidden_in(1)
        send_back(BWD, 0)
        both(1)
        scaled0 = cross_start(0, sec_in[0])
        send_back(BWD, 1)
        finish(0, scaled0)
        out_partial(0)
        scaled1 = cross_start(1, sec_in[1])
        send_back(FWD, 0)
        finish(1, scaled1)
        out_partial(1)
        send_back(FWD, 1)
        weight_grads()
        for m in range(micro):
            out_ref[m] = layer_out(m, sec_in[m])

    for m in range(micro):
        for kind in (FWD, BWD):
            def drain(block):
                chunk_copy(kind, m, block, me).wait_send()
                cross_copy(kind, m, block, me, own_cols).wait_send()
                back_copy(kind, m, block, me).wait_send()

            each_peer(drain)
            cross_copy(kind, m, me, me, own_cols).wait_send()
            for c in range(SPLIT):
                away_copy(kind, m, c).wait_send()
        section_copy(m).wait_send()
        sum_copy(SQUARE, m).wait_send()
        sum_copy(CROSS, m).wait_send()


def copy_out(out_in, gin_in, gout_in, out_ref, gin_ref, gout_ref, sem):
    pairs = ((gin_in, gin_ref), (gout_in, gout_ref), (out_in, out_ref))
    copies = [pltpu.make_async_copy(a, b, sem.at[i]) for i, (a, b) in enumerate(pairs)]
    for copy in copies:
        copy.start()
    for copy in copies:
        copy.wait()


def on_device(boundary, norm_gain, gate_prob, expert_ids, slot_ids, weight_in, weight_out):
    experts = lax.axis_size("expert")
    micro, tok, half = boundary.shape[1:]
    full, hidden_half = weight_in.shape[2:]
    cap = 2 * tok // experts
    pad = -(-cap // 16) * 16
    total = experts * pad
    mid_type = F32 if total <= 512 else BF16
    vmem = pl.BlockSpec(memory_space=pltpu.VMEM)
    anywhere = pl.BlockSpec(memory_space=pl.ANY)
    per_block = pltpu.SemaphoreType.DMA((2, micro, experts))
    per_pair = pltpu.SemaphoreType.DMA((2, micro))
    per_piece = pltpu.SemaphoreType.DMA((2, micro, SPLIT))
    per_micro = pltpu.SemaphoreType.DMA((micro,))
    pieces = pltpu.VMEM((2, micro, total, half), BF16)
    tokens = pltpu.VMEM((micro, tok, half), BF16)
    sums = pltpu.VMEM((2, micro, 8, tok), F32)
    out, grad_in, grad_out = pl.pallas_call(
        functools.partial(kernel, experts, cap, pad),
        out_shape=(
            pltpu.VMEM((micro, tok, half), BF16),
            pltpu.VMEM((full, hidden_half), BF16),
            pltpu.VMEM((hidden_half, full), BF16),
        ),
        in_specs=[vmem] * 5 + [anywhere] * 2,
        out_specs=(vmem, vmem, vmem),
        scratch_shapes=[
            pltpu.VMEM((micro, total, tok), BF16),
            pieces,
            pltpu.VMEM((2, micro * total, full), BF16),
            pltpu.VMEM((micro * total, full), BF16),
            pltpu.VMEM((micro * total, hidden_half), BF16),
            pltpu.VMEM((micro * total, hidden_half), BF16),
            pltpu.VMEM((micro * total, hidden_half), mid_type),
            pieces,
            pieces,
            pieces,
            pieces,
            tokens,
            tokens,
            sums,
            sums,
            pltpu.VMEM((full, hidden_half), BF16),
            pltpu.VMEM((hidden_half, full), BF16),
            pltpu.SemaphoreType.DMA((2,)),
            per_block, per_block,
            per_block, per_block,
            per_piece, per_piece,
            per_block, per_block,
            per_micro, per_micro,
            per_pair, per_pair,
        ],
        compiler_params=pltpu.CompilerParams(
            collective_id=0, has_side_effects=True, vmem_limit_bytes=VMEM_LIMIT
        ),
    )(
        boundary[0], norm_gain, gate_prob[0], expert_ids[0], slot_ids[0],
        weight_in[0, 0], weight_out[0, 0],
    )
    results = (out, grad_in, grad_out)
    out, grad_in, grad_out = pl.pallas_call(
        copy_out,
        out_shape=[jax.ShapeDtypeStruct(x.shape, x.dtype) for x in results],
        in_specs=[vmem] * 3,
        out_specs=[anywhere] * 3,
        scratch_shapes=[pltpu.SemaphoreType.DMA((3,))],
        compiler_params=pltpu.CompilerParams(vmem_limit_bytes=COPY_LIMIT),
    )(*results)
    return (out[None], grad_in[None, None], grad_out[None, None])


def solution(mesh):
    placed = (
        P("section", None, "expert", "head"),
        P("section", None),
        P("section", None, "expert"),
        P("section", None, "expert"),
        P("section", None, "expert"),
        P("section", "expert", None, "head"),
        P("section", "expert", "head", None),
    )
    return jax.shard_map(
        on_device,
        mesh=mesh,
        in_specs=placed,
        out_specs=(
            P("section", None, "expert", "head"),
            P("section", "expert", None, "head"),
            P("section", "expert", "head", None),
        ),
        check_vma=False,
    )
```

```python
import functools

import jax
import jax.numpy as jnp
from jax import lax
from jax.experimental import pallas as pl
from jax.experimental.pallas import tpu as pltpu
from jax.sharding import PartitionSpec as P

EPSILON = 1e-06
ROOT_COEF = 0.7978845608
CUBE_COEF = 0.044715
MESH = pl.DeviceIdType.MESH
BF16 = jnp.bfloat16
F32 = jnp.float32
FWD, BWD = 0, 1
SQUARE, CROSS = 0, 1
COLS = 256
SPLIT = 2
VMEM_LIMIT = 56 * 2**20
COPY_LIMIT = 2**20


def activate(pre_act):
    tangent = jnp.tanh(ROOT_COEF * (pre_act + CUBE_COEF * pre_act * pre_act * pre_act))
    act_value = 0.5 * pre_act * (1.0 + tangent)
    act_slope = 0.5 * (1.0 + tangent) + 0.5 * pre_act * (1.0 - tangent * tangent) * ROOT_COEF * (
        1.0 + 3.0 * CUBE_COEF * pre_act * pre_act
    )
    return (act_value, act_slope)


def dot(left, right, dims=((1,), (0,))):
    return lax.dot_general(left, right, (dims, ((), ())), preferred_element_type=F32)


NT = ((1,), (1,))
TN = ((0,), (0,))


def kernel(
    experts, cap, pad,
    local_ref, gain_ref, prob_ref, ids_ref, slots_ref, win_hbm, wout_hbm,
    out_ref, gin_ref, gout_ref,
    tab, send, rows, normed, act, gpre, mid, keep, away, recvp, back, sec_src, sec_in, xsend, xrecv,
    win_ref, wout_ref, load_sem, turn,
    s1, r1, s2, r2, s3, r3, s4, r4, s5, r5, s6, r6,
):
    win_load = pltpu.make_async_copy(win_hbm, win_ref, load_sem.at[0])
    wout_load = pltpu.make_async_copy(wout_hbm, wout_ref, load_sem.at[1])
    win_load.start()
    wout_load.start()
    sec, me, head = lax.axis_index("section"), lax.axis_index("expert"), lax.axis_index("head")
    other = 1 - head
    micro, tok, half = local_ref.shape
    full = 2 * half
    total = experts * pad
    hidden_half = win_ref.shape[1]
    chunks = hidden_half // COLS
    own_cols = pl.ds(pl.multiple_of(head * half, 128), half)
    other_cols = pl.ds(pl.multiple_of(other * half, 128), half)

    barrier = pltpu.get_barrier_semaphore()

    def each_peer(action):
        def step(k, carry):
            action(lax.rem(me + k, experts))
            return carry

        lax.fori_loop(1, experts, step, 0)

    def greet(d):
        for h in range(2):
            pl.semaphore_signal(
                barrier, inc=1, device_id={"expert": d, "head": h}, device_id_type=MESH
            )

    each_peer(greet)
    pl.semaphore_signal(barrier, inc=1, device_id={"head": other}, device_id_type=MESH)
    pl.semaphore_signal(barrier, inc=1, device_id={"section": 1 - sec}, device_id_type=MESH)

    def slot_rows(index):
        return pl.ds(pl.multiple_of(index * pad, pad), pad)

    def micro_rows(m, index):
        return pl.ds(pl.multiple_of(m * total + index * pad, pad), pad)

    def span(m):
        return slice(m * total, (m + 1) * total)

    eye = lax.broadcasted_iota(jnp.int32, (tok, tok), 0) == lax.broadcasted_iota(
        jnp.int32, (tok, tok), 1
    )

    def to_col(row):
        return jnp.sum(jnp.where(eye, row, 0.0), axis=1, keepdims=True)

    def to_row(col):
        return jnp.sum(jnp.where(eye, col, 0.0), axis=0, keepdims=True)

    for m in range(micro):
        ids, slots = ids_ref[m : m + 1, :], slots_ref[m : m + 1, :]
        target = jnp.where(slots < cap, ids * pad + slots, -1)
        hit = target == lax.broadcasted_iota(jnp.int32, (total, tok), 0)
        tab[m] = jnp.where(hit, 1.0, 0.0).astype(BF16)
    prob = [to_col(prob_ref[m : m + 1, :]) for m in range(micro)]
    gain = gain_ref[...]
    gain_half = gain_ref[:, own_cols]

    def chunk_copy(kind, m, dst, came_from):
        return pltpu.make_async_remote_copy(
            src_ref=send.at[kind, m, slot_rows(dst), :],
            dst_ref=rows.at[kind, micro_rows(m, came_from), own_cols],
            send_sem=s1.at[kind, m, dst],
            recv_sem=r1.at[kind, m, came_from],
            device_id={"expert": dst},
            device_id_type=MESH,
        )

    def cross_copy(kind, m, dst, came_from, cols):
        return pltpu.make_async_remote_copy(
            src_ref=send.at[kind, m, slot_rows(dst), :],
            dst_ref=rows.at[kind, micro_rows(m, came_from), cols],
            send_sem=s2.at[kind, m, dst],
            recv_sem=r2.at[kind, m, came_from],
            device_id={"expert": dst, "head": other},
            device_id_type=MESH,
        )

    def place(kind, m, tokens):
        send[kind, m] = dot(tab[m], tokens).astype(BF16)

    def dispatch(kind, m):
        def both_heads(d):
            cross_copy(kind, m, d, me, own_cols).start()
            chunk_copy(kind, m, d, me).start()

        each_peer(both_heads)
        cross_copy(kind, m, me, me, own_cols).start()
        rows[kind, micro_rows(m, me), own_cols] = send[kind, m, slot_rows(me), :]

    def arrived(kind, m):
        def both_heads(block):
            chunk_copy(kind, m, block, block).wait_recv()
            cross_copy(kind, m, block, block, other_cols).wait_recv()

        cross_copy(kind, m, me, me, other_cols).wait_recv()
        each_peer(both_heads)

    def piece(c):
        return slice(c * (total // SPLIT), (c + 1) * (total // SPLIT))

    def piece_of(m, c):
        return slice(m * total + c * (total // SPLIT), m * total + (c + 1) * (total // SPLIT))

    def away_copy(kind, m, c):
        return pltpu.make_async_remote_copy(
            src_ref=away.at[kind, m, piece(c), :],
            dst_ref=recvp.at[kind, m, piece(c), :],
            send_sem=s3.at[kind, m, c],
            recv_sem=r3.at[kind, m, c],
            device_id={"head": other},
            device_id_type=MESH,
        )

    def back_copy(kind, m, dst, came_from):
        return pltpu.make_async_remote_copy(
            src_ref=keep.at[kind, m, slot_rows(dst), :],
            dst_ref=back.at[kind, m, slot_rows(came_from), :],
            send_sem=s4.at[kind, m, dst],
            recv_sem=r4.at[kind, m, came_from],
            device_id={"expert": dst},
            device_id_type=MESH,
        )

    def send_back(kind, m):
        for c in range(SPLIT):
            away_copy(kind, m, c).wait_recv()
            summed = keep[kind, m, piece(c), :].astype(F32) + recvp[kind, m, piece(c), :].astype(F32)
            keep[kind, m, piece(c), :] = summed.astype(BF16)

            def one(dst, carry):
                @pl.when(dst != me)
                def _():
                    back_copy(kind, m, dst, me).start()

                return carry

            lax.fori_loop(c * experts // SPLIT, (c + 1) * experts // SPLIT, one, 0)
        back[kind, m, slot_rows(me), :] = keep[kind, m, slot_rows(me), :]

    def collect(kind, m):
        each_peer(lambda block: back_copy(kind, m, block, block).wait_recv())
        return dot(tab[m], back[kind, m], TN)

    def section_copy(m):
        return pltpu.make_async_remote_copy(
            src_ref=sec_src.at[m],
            dst_ref=sec_in.at[m],
            send_sem=s5.at[m],
            recv_sem=r5.at[m],
            device_id={"section": 1 - sec},
            device_id_type=MESH,
        )

    def sum_copy(what, m):
        return pltpu.make_async_remote_copy(
            src_ref=xsend.at[what, m],
            dst_ref=xrecv.at[what, m],
            send_sem=s6.at[what, m],
            recv_sem=r6.at[what, m],
            device_id={"head": other},
            device_id_type=MESH,
        )

    def sum_start(what, m, col):
        xsend[what, m] = jnp.broadcast_to(to_row(col), (8, tok))
        sum_copy(what, m).start()

    def sum_done(what, m):
        sum_copy(what, m).wait_recv()
        return to_col(xsend[what, m, 0:1, :] + xrecv[what, m, 0:1, :])

    def square_start(m, tokens):
        values = tokens.astype(F32)
        sum_start(SQUARE, m, jnp.sum(values * values, axis=1, keepdims=True))

    def normalize(m):
        values = rows[FWD, span(m), :].astype(F32)
        inv_scale = lax.rsqrt(jnp.mean(values * values, axis=-1, keepdims=True) + EPSILON)
        normed[span(m), :] = (values * inv_scale * gain).astype(BF16)

    def each_chunk(action):
        def step(c, carry):
            action(pl.ds(pl.multiple_of(c * COLS, COLS), COLS))
            return carry

        lax.fori_loop(0, chunks, step, 0)

    def out_partial(m):
        for c in range(SPLIT):
            away[FWD, m, piece(c), :] = dot(act[piece_of(m, c), :], wout_ref[:, other_cols]).astype(
                BF16
            )
            away_copy(FWD, m, c).start()
        keep[FWD, m] = dot(act[span(m), :], wout_ref[:, own_cols]).astype(BF16)

    def grad_partial(m):
        for c in range(SPLIT):
            away[BWD, m, piece(c), :] = dot(gpre[piece_of(m, c), :], win_ref[other_cols, :], NT).astype(
                BF16
            )
            away_copy(BWD, m, c).start()
        keep[BWD, m] = dot(gpre[span(m), :], win_ref[own_cols, :], NT).astype(BF16)

    def layer_out(m, tokens):
        return (tokens.astype(F32) + prob[m] * collect(FWD, m)).astype(BF16)

    def sent_grad(m, cot):
        return (prob[m] * cot.astype(F32)).astype(BF16)

    def cross_start(m, tokens):
        scaled = gain_half * collect(BWD, m)
        sum_start(CROSS, m, jnp.sum(scaled * tokens.astype(F32), axis=1, keepdims=True))
        return scaled

    def layer_grad(m, tokens, cot, scaled):
        inv = lax.rsqrt(sum_done(SQUARE, m) / full + EPSILON)
        cross = sum_done(CROSS, m)
        values = tokens.astype(F32)
        return (
            cot.astype(F32) + inv * scaled - values * (inv * inv * inv * cross / full)
        ).astype(BF16)

    def weight_grads():
        def first(c, carry):
            part = pl.ds(pl.multiple_of(c * COLS, COLS), COLS)
            gin_ref[part, :] = dot(normed[:, part], gpre[...], TN).astype(BF16)
            return carry

        lax.fori_loop(0, full // COLS, first, 0)

        def second(part):
            gout_ref[part, :] = dot(act[:, part], rows[BWD], TN).astype(BF16)

        each_chunk(second)


    @pl.when(sec == 0)
    def _():
        for m in range(micro):
            place(FWD, m, local_ref[m])
        pl.semaphore_wait(barrier, 2 * experts)
        for m in range(micro):
            dispatch(FWD, m)
        for m in range(micro):
            square_start(m, local_ref[m])
        win_load.wait()
        wout_load.wait()

        def forward(m):
            arrived(FWD, m)
            pl.semaphore_signal(
                turn.at[m], inc=1, device_id={"section": 1 - sec}, device_id_type=MESH
            )
            normalize(m)

            def chunk(part):
                pre = dot(normed[span(m), :], win_ref[:, part])
                value, slope = activate(pre)
                act[span(m), part] = value.astype(BF16)
                mid[span(m), part] = slope.astype(mid.dtype)

            each_chunk(chunk)
            out_partial(m)

        def hidden(m):
            sec_src[m] = layer_out(m, local_ref[m])
            section_copy(m).start()

        forward(0)
        send_back(FWD, 0)
        forward(1)
        hidden(0)
        send_back(FWD, 1)
        hidden(1)

        def grad_in(m):
            section_copy(m).wait_recv()
            place(BWD, m, sent_grad(m, sec_in[m]))
            dispatch(BWD, m)

        def backward(m):
            arrived(BWD, m)

            def chunk(part):
                grad_act = dot(rows[BWD, span(m), :], wout_ref[part, :], NT)
                gpre[span(m), part] = (grad_act * mid[span(m), part].astype(F32)).astype(BF16)

            each_chunk(chunk)
            grad_partial(m)

        grad_in(0)
        backward(0)
        grad_in(1)
        send_back(BWD, 0)
        backward(1)
        scaled0 = cross_start(0, local_ref[0])
        send_back(BWD, 1)
        out_ref[0] = layer_grad(0, local_ref[0], sec_in[0], scaled0)
        weight_grads()
        scaled1 = cross_start(1, local_ref[1])
        out_ref[1] = layer_grad(1, local_ref[1], sec_in[1], scaled1)

    @pl.when(sec != 0)
    def _():
        for m in range(micro):
            place(BWD, m, sent_grad(m, local_ref[m]))
        pl.semaphore_wait(barrier, 2 * experts)
        win_load.wait()
        wout_load.wait()
        for m in range(micro):
            pl.semaphore_wait(turn.at[m], 1)
            dispatch(BWD, m)

        def early_grad(m):
            arrived(BWD, m)

            def early(part):
                grad_act = dot(rows[BWD, span(m), :], wout_ref[part, :], NT)
                mid[span(m), part] = grad_act.astype(mid.dtype)

            each_chunk(early)

        for m in range(micro):
            early_grad(m)

        def hidden_in(m):
            section_copy(m).wait_recv()
            place(FWD, m, sec_in[m])
            dispatch(FWD, m)
            square_start(m, sec_in[m])

        def both(m):
            arrived(FWD, m)
            normalize(m)

            def chunk(part):
                pre = dot(normed[span(m), :], win_ref[:, part])
                value, slope = activate(pre)
                act[span(m), part] = value.astype(BF16)
                gpre[span(m), part] = (mid[span(m), part].astype(F32) * slope).astype(BF16)

            each_chunk(chunk)
            grad_partial(m)

        def finish(m, scaled):
            sec_src[m] = layer_grad(m, sec_in[m], local_ref[m], scaled)
            section_copy(m).start()

        hidden_in(0)
        both(0)
        hidden_in(1)
        send_back(BWD, 0)
        both(1)
        scaled0 = cross_start(0, sec_in[0])
        send_back(BWD, 1)
        finish(0, scaled0)
        out_partial(0)
        scaled1 = cross_start(1, sec_in[1])
        send_back(FWD, 0)
        finish(1, scaled1)
        out_partial(1)
        send_back(FWD, 1)
        weight_grads()
        for m in range(micro):
            out_ref[m] = layer_out(m, sec_in[m])

    for m in range(micro):
        for kind in (FWD, BWD):
            def drain(block):
                chunk_copy(kind, m, block, me).wait_send()
                cross_copy(kind, m, block, me, own_cols).wait_send()
                back_copy(kind, m, block, me).wait_send()

            each_peer(drain)
            cross_copy(kind, m, me, me, own_cols).wait_send()
            for c in range(SPLIT):
                away_copy(kind, m, c).wait_send()
        section_copy(m).wait_send()
        sum_copy(SQUARE, m).wait_send()
        sum_copy(CROSS, m).wait_send()


def copy_out(out_in, gin_in, gout_in, out_ref, gin_ref, gout_ref, sem):
    pairs = ((gin_in, gin_ref), (gout_in, gout_ref), (out_in, out_ref))
    copies = [pltpu.make_async_copy(a, b, sem.at[i]) for i, (a, b) in enumerate(pairs)]
    for copy in copies:
        copy.start()
    for copy in copies:
        copy.wait()


def on_device(boundary, norm_gain, gate_prob, expert_ids, slot_ids, weight_in, weight_out):
    experts = lax.axis_size("expert")
    micro, tok, half = boundary.shape[1:]
    full, hidden_half = weight_in.shape[2:]
    cap = 2 * tok // experts
    pad = -(-cap // 16) * 16
    total = experts * pad
    mid_type = F32 if total <= 512 else BF16
    vmem = pl.BlockSpec(memory_space=pltpu.VMEM)
    anywhere = pl.BlockSpec(memory_space=pl.ANY)
    per_block = pltpu.SemaphoreType.DMA((2, micro, experts))
    per_pair = pltpu.SemaphoreType.DMA((2, micro))
    per_piece = pltpu.SemaphoreType.DMA((2, micro, SPLIT))
    per_micro = pltpu.SemaphoreType.DMA((micro,))
    pieces = pltpu.VMEM((2, micro, total, half), BF16)
    tokens = pltpu.VMEM((micro, tok, half), BF16)
    sums = pltpu.VMEM((2, micro, 8, tok), F32)
    out, grad_in, grad_out = pl.pallas_call(
        functools.partial(kernel, experts, cap, pad),
        out_shape=(
            pltpu.VMEM((micro, tok, half), BF16),
            pltpu.VMEM((full, hidden_half), BF16),
            pltpu.VMEM((hidden_half, full), BF16),
        ),
        in_specs=[vmem] * 5 + [anywhere] * 2,
        out_specs=(vmem, vmem, vmem),
        scratch_shapes=[
            pltpu.VMEM((micro, total, tok), BF16),
            pieces,
            pltpu.VMEM((2, micro * total, full), BF16),
            pltpu.VMEM((micro * total, full), BF16),
            pltpu.VMEM((micro * total, hidden_half), BF16),
            pltpu.VMEM((micro * total, hidden_half), BF16),
            pltpu.VMEM((micro * total, hidden_half), mid_type),
            pieces,
            pieces,
            pieces,
            pieces,
            tokens,
            tokens,
            sums,
            sums,
            pltpu.VMEM((full, hidden_half), BF16),
            pltpu.VMEM((hidden_half, full), BF16),
            pltpu.SemaphoreType.DMA((2,)),
            pltpu.SemaphoreType.REGULAR((micro,)),
            per_block, per_block,
            per_block, per_block,
            per_piece, per_piece,
            per_block, per_block,
            per_micro, per_micro,
            per_pair, per_pair,
        ],
        compiler_params=pltpu.CompilerParams(
            collective_id=0, has_side_effects=True, vmem_limit_bytes=VMEM_LIMIT
        ),
    )(
        boundary[0], norm_gain, gate_prob[0], expert_ids[0], slot_ids[0],
        weight_in[0, 0], weight_out[0, 0],
    )
    results = (out, grad_in, grad_out)
    out, grad_in, grad_out = pl.pallas_call(
        copy_out,
        out_shape=[jax.ShapeDtypeStruct(x.shape, x.dtype) for x in results],
        in_specs=[vmem] * 3,
        out_specs=[anywhere] * 3,
        scratch_shapes=[pltpu.SemaphoreType.DMA((3,))],
        compiler_params=pltpu.CompilerParams(vmem_limit_bytes=COPY_LIMIT),
    )(*results)
    return (out[None], grad_in[None, None], grad_out[None, None])


def solution(mesh):
    placed = (
        P("section", None, "expert", "head"),
        P("section", None),
        P("section", None, "expert"),
        P("section", None, "expert"),
        P("section", None, "expert"),
        P("section", "expert", None, "head"),
        P("section", "expert", "head", None),
    )
    return jax.shard_map(
        on_device,
        mesh=mesh,
        in_specs=placed,
        out_specs=(
            P("section", None, "expert", "head"),
            P("section", "expert", None, "head"),
            P("section", "expert", "head", None),
        ),
        check_vma=False,
    )
```
